512 devices in a mesh: leaf: 32 (over x, y), front: 16 (over z, core).
Axes of the slice: x: 4, y: 8, z: 8, core: 2. Of those that a mesh axis runs over, the one named last changes fastest.
Arguments:
- child_pivot: float32 [32, 512, 512], P('leaf', 'front')
- child_panel: float32 [32, 2048, 512], P('leaf', 'front'), may hold values from -0.9 to 0.9
- anc_front: float32 [32, 16, 512, 512], P('leaf', 'front')
- dest_list: int32 [32, 16], replicated, may hold values from 0 to 31, as said below
- col_list: int32 [32, 16], replicated, may hold values from 0 to 3, as said below
- row_list: int32 [32, 16], replicated, may hold values from 0 to 3, as said below
Outputs:
- child_lower: float32 [32, 512, 512], P('leaf', 'front')
- child_factor: float32 [32, 2048, 512], P('leaf', 'front')
- anc_factor: float32 [32, 16, 512, 512], P('leaf', 'front')
The draws below stay inside these ranges and needn't reach their ends.
Inputs may be any that keep to these rules, and one draw needn't show every extreme that they name: dest_list[g, j] is g with exactly one bit of its index flipped; every group that row g names is named there by exactly 4 column blocks, so row g names 4 different groups. `col_list`: column blocks of one group that name the same group in dest_list have different entries here. row_list[g, f] is 1 or more for f < 4.
All inputs are finite; a program needn't handle non-finite values.
Results may differ from the reference program's by a relative error of at most 0.0001.
Values sent between devices are 32-bit elements; how exact they have to be, the bound alone decides.
No kernel may reach another device: no remote copies, remote signals or barrier semaphores. Data moves between devices by JAX's collectives and lax.ppermute only.
A program may use at most 64 MiB of HBM per device.

```python
import math
import jax
import jax.numpy as jnp
from jax import lax

BLK = 128
SCOL = 512
ARB = 4
CB = 4
U = 2048
N_LEAF = 32
N_FRONT = 16


def coupled_blocks(key, count):
    keys = jax.random.split(key, 6)
    spacing = float(SCOL) ** (-1.0 / 3.0)
    reach = 0.5 * spacing
    shape = (count, SCOL)
    across = jax.random.uniform(keys[0], shape, jnp.float32)
    along = jax.random.uniform(keys[1], shape, jnp.float32)
    height = jax.random.uniform(keys[2], shape, jnp.float32)
    signs = jnp.where(jax.random.bernoulli(keys[4], 0.5, shape), 1.0, -1.0).astype(jnp.float32)
    scales = jnp.exp(jax.random.uniform(keys[3], shape, jnp.float32, math.log(0.6), math.log(1.6)))
    gap = (across[:, :, None] - across[:, None, :]) ** 2
    gap = gap + (along[:, :, None] - along[:, None, :]) ** 2
    gap = gap + (height[:, :, None] - height[:, None, :]) ** 2
    kernel = jnp.exp(-jnp.sqrt(gap) / reach)
    weights = scales * signs
    coupled = weights[:, :, None] * weights[:, None, :] * kernel
    extra = jax.random.uniform(keys[5], shape, jnp.float32, 0.3, 0.6)
    ids = jnp.arange(SCOL)
    on_diagonal = ids[:, None] == ids[None, :]
    return coupled + jnp.where(on_diagonal[None], extra[:, :, None], 0.0)


def draw_child_pivot(key, part):
    return coupled_blocks(jax.random.fold_in(key, 1), N_LEAF).astype(jnp.float32)


def draw_anc_front(key, part):
    value_key, pivot_key = jax.random.split(jax.random.fold_in(key, 2))
    shape = (N_LEAF, N_FRONT, ARB * BLK, SCOL)
    values = jax.random.normal(value_key, shape, jnp.float32)
    pivot = coupled_blocks(pivot_key, N_LEAF).reshape(N_LEAF, SCOL // BLK, BLK, SCOL)
    return values.at[:, :SCOL // BLK, :BLK, :].set(pivot).astype(jnp.float32)


def shuffle_row(key):
    return jax.random.permutation(key, N_FRONT)


def route_tables(key):
    keys = jax.random.split(jax.random.fold_in(key, 7), 3)
    width_blocks = SCOL // BLK
    named = N_FRONT // width_blocks
    depth = int(N_LEAF).bit_length() - 1
    groups = jnp.arange(N_LEAF, dtype=jnp.int32)
    bit_ids = jnp.arange(depth, dtype=jnp.int32)
    bit_score = jax.random.randint(keys[0], (N_LEAF, depth), 0, 4096) * depth + bit_ids[None, :]
    bits = lax.top_k(bit_score, named)[1].astype(jnp.int32)
    owners = jnp.bitwise_xor(groups[:, None], jnp.left_shift(jnp.ones_like(bits), bits))
    dest = jnp.repeat(owners, width_blocks, axis=1)
    col_ids = jnp.arange(width_blocks, dtype=jnp.int32)
    col_score = jax.random.randint(keys[1], (N_LEAF, named, width_blocks), 0, 4096) * width_blocks + col_ids
    cols = jnp.argsort(col_score, axis=2, stable=True).astype(jnp.int32).reshape(N_LEAF, N_FRONT)
    orders = jax.vmap(shuffle_row)(jax.random.split(keys[2], N_LEAF))
    dest = jnp.take_along_axis(dest, orders, axis=1)
    cols = jnp.take_along_axis(cols, orders, axis=1)
    return (dest.astype(jnp.int32), cols.astype(jnp.int32))


def draw_dest_list(key, part):
    return route_tables(key)[0]


def draw_col_list(key, part):
    return route_tables(key)[1]


def draw_row_list(key, part):
    lowest = (jnp.arange(N_FRONT) < SCOL // BLK).astype(jnp.int32)
    lowest = jnp.broadcast_to(lowest[None, :], (N_LEAF, N_FRONT))
    return jax.random.randint(jax.random.fold_in(key, 9), (N_LEAF, N_FRONT), lowest, ARB).astype(jnp.int32)


def levels(stream_key, extent, pieces, low, largest):
    def one(axis_at, blocks):
        steps = jax.random.uniform(jax.random.fold_in(jax.random.fold_in(stream_key, 6), axis_at), (blocks,), jnp.float32, low / len(pieces), largest / len(pieces))
        return jnp.repeat(jnp.exp(steps), extent[axis_at] // blocks).reshape((-1,) + (1,) * (len(extent) - axis_at - 1))

    gain = one(*pieces[0])
    for cut in pieces[1:]:
        gain = gain * one(*cut)
    return gain


def centred(rng, dims, width, most, shards=(), held_as=jnp.bfloat16):
    drawn = width * jax.random.normal(rng, dims, jnp.float32)
    if shards:
        drawn = drawn * levels(rng, dims, shards, -0.22, 0.18)
    return jnp.clip(drawn, -most, most).astype(held_as)


def setup_inputs(seed: int = 0) -> dict:
    key_list = jax.random.split(jax.random.key(seed), 7)
    child_pivot = draw_child_pivot(jax.random.fold_in(key_list[6], 71), 0)
    child_panel = centred(key_list[1], (N_LEAF, U, SCOL), 0.15, 0.9, ((0, 32), (1, 16)), jnp.float32)
    anc_front = draw_anc_front(jax.random.fold_in(key_list[6], 71), 0)
    dest_list = draw_dest_list(jax.random.fold_in(key_list[6], 71), 0)
    col_list = draw_col_list(jax.random.fold_in(key_list[6], 71), 0)
    row_list = draw_row_list(jax.random.fold_in(key_list[6], 71), 0)
    return dict(child_pivot=child_pivot, child_panel=child_panel, anc_front=anc_front, dest_list=dest_list, col_list=col_list, row_list=row_list)


def place_blocks(acc, update, targets, cols, rows):
    blocks = update.reshape(N_FRONT, BLK, N_FRONT, BLK).transpose(0, 2, 1, 3)
    front_ids = jnp.arange(N_FRONT, dtype=jnp.int32)
    return acc.at[targets[None, :], front_ids[:, None], rows[:, None], :, cols[None, :], :].add(blocks)

def reference(child_pivot, child_panel, anc_front, dest_list, col_list, row_list):

    def child_step(acc, inputs):
        pivot, panel, targets, cols, rows = inputs
        lower = jnp.linalg.cholesky(pivot)
        factor = lax.linalg.triangular_solve(lower, panel, left_side=False, lower=True, transpose_a=True)
        update = jnp.dot(factor.astype(jnp.float32), factor.T.astype(jnp.float32), precision=lax.Precision.HIGHEST, preferred_element_type=jnp.float32)
        acc = place_blocks(acc, update, targets, cols, rows)
        return (acc, (lower, factor))
    start = jnp.zeros((N_LEAF, N_FRONT, ARB, BLK, CB, BLK), jnp.float32)
    received, (child_lower, child_factor) = lax.scan(child_step, start, (child_pivot, child_panel, dest_list, col_list, row_list))
    assembled = anc_front - received.reshape(N_LEAF, N_FRONT, ARB * BLK, SCOL)
    front_ids = jnp.arange(N_FRONT, dtype=jnp.int32)
    row_ids = jnp.arange(ARB * BLK, dtype=jnp.int32)
    mask = (front_ids < CB)[:, None, None] & (row_ids < BLK)[None, :, None]

    def ancestor_step(front):
        pivot = front[:CB, :BLK, :].reshape(SCOL, SCOL)
        lower = jnp.linalg.cholesky(pivot)
        rows_all = front.reshape(N_FRONT * ARB * BLK, SCOL)
        solved = lax.linalg.triangular_solve(lower, rows_all, left_side=False, lower=True, transpose_a=True)
        solved = solved.reshape(N_FRONT, ARB * BLK, SCOL)
        padded = jnp.zeros((N_FRONT, ARB * BLK, SCOL), jnp.float32).at[:CB, :BLK, :].set(lower.reshape(CB, BLK, SCOL))
        return jnp.where(mask, padded, solved)
    anc_factor = lax.map(ancestor_step, assembled)
    return (child_lower, child_factor, anc_factor)
```

```python
import jax
import jax.numpy as jnp
from jax import lax
from jax.experimental import pallas as pl
from jax.experimental.pallas import tpu as pltpu
from jax.sharding import PartitionSpec as P

F32 = jnp.float32
BLK = 128
SUB = 8


def dot(a, b, ca=1, cb=0):
    return lax.dot_general(
        a,
        b,
        (((ca,), (cb,)), ((), ())),
        precision=lax.Precision.HIGHEST,
        preferred_element_type=F32,
    )


def split3(x):
    high = x.astype(jnp.bfloat16).astype(F32)
    rest = x - high
    mid = rest.astype(jnp.bfloat16).astype(F32)
    return high, mid, rest - mid


def eliminate(m_ref, k):
    base = SUB * k
    rows = m_ref[base : base + SUB, :]
    ra = [jnp.broadcast_to(rows[i : i + 1, :BLK], (SUB, BLK)) for i in range(SUB)]
    rb = [jnp.broadcast_to(rows[i : i + 1, BLK:], (SUB, BLK)) for i in range(SUB)]
    d = {}
    for i in range(SUB):
        for j in range(i, SUB):
            d[i, j] = jnp.broadcast_to(ra[i][:, base + j : base + j + 1], (SUB, BLK))
    sub = lax.broadcasted_iota(jnp.int32, (SUB, BLK), 0)
    ua_all = ub_all = None
    for q in range(SUB):
        s = lax.rsqrt(d[q, q])
        ua = ra[q] * s
        ub = rb[q] * s
        low = {i: d[q, i] * s for i in range(q + 1, SUB)}
        for i in range(q + 1, SUB):
            for j in range(i, SUB):
                d[i, j] = d[i, j] - low[i] * low[j]
        for i in range(q + 1, SUB):
            ra[i] = ra[i] - low[i] * ua
            rb[i] = rb[i] - low[i] * ub
        ua_all = ua if q == 0 else jnp.where(sub == q, ua, ua_all)
        ub_all = ub if q == 0 else jnp.where(sub == q, ub, ub_all)
    u = jnp.concatenate([ua_all, ub_all], 1)
    m_ref[base : base + SUB, :] = u
    if base + SUB < BLK:
        hi, mi, lo = split3(u)
        ah, am, al = hi[:, :BLK], mi[:, :BLK], lo[:, :BLK]
        left = jnp.concatenate([ah, ah, am, ah, al, am], 0).astype(jnp.bfloat16)
        right = jnp.concatenate([hi, mi, hi, lo, hi, mi], 0).astype(jnp.bfloat16)
        upd = lax.dot_general(
            left, right, (((0,), (0,)), ((), ())), preferred_element_type=F32
        )
        m_ref[base + SUB :, :] = m_ref[base + SUB :, :] - upd[base + SUB :, :]


def factor(t, l_ref, x_ref, m_ref):
    n = t.shape[0]
    ri = lax.broadcasted_iota(jnp.int32, (BLK, BLK), 0)
    ci = lax.broadcasted_iota(jnp.int32, (BLK, BLK), 1)
    cols = lax.broadcasted_iota(jnp.int32, (BLK, n), 1)
    x_ref[...] = jnp.zeros((n, n), F32)
    l_ref[...] = jnp.zeros((n, n), F32)

    def step(b, carry):
        r0 = pl.multiple_of(b * BLK, BLK)
        m_ref[:, :BLK] = t[pl.ds(r0, BLK), pl.ds(r0, BLK)]
        m_ref[:, BLK:] = (ri == ci).astype(F32)
        for k in range(BLK // SUB):
            eliminate(m_ref, k)
        inv = m_ref[:, BLK:]
        diag = jnp.where(ci >= ri, m_ref[:, :BLK], 0.0)
        u = dot(inv, t[pl.ds(r0, BLK), :])
        wide = jnp.concatenate([diag] * (n // BLK), 1)
        u = jnp.where(cols >= r0 + BLK, u, jnp.where(cols < r0, 0.0, wide))
        l_ref[:, pl.ds(r0, BLK)] = u.T
        s = dot(l_ref[pl.ds(r0, BLK), :], x_ref[...])
        here = (cols >= r0) & (cols < r0 + BLK)
        wide_inv = jnp.concatenate([inv] * (n // BLK), 1)
        x_ref[pl.ds(r0, BLK), :] = jnp.where(here, wide_inv, 0.0) - dot(inv, s)
        t[...] = t[...] - dot(u, u, 0, 0)
        return carry

    lax.fori_loop(0, n // BLK, step, 0)


def child_kernel(ids, own, other, rows_out, x_ref, t, l_ref, m_ref):
    front = ids[1]
    z, core = front // 2, front % 2
    slab = rows_out.shape[0]
    for q in range(own.shape[0] // slab):
        at = 2 * slab * (z ^ q)
        mine = pl.multiple_of(at + slab * core, slab)
        theirs = pl.multiple_of(at + slab * (1 - core), slab)
        t[pl.ds(mine, slab), :] = own[slab * q : slab * (q + 1), :]
        t[pl.ds(theirs, slab), :] = other[slab * q : slab * (q + 1), :]
    factor(t, l_ref, x_ref, m_ref)
    rows_out[...] = l_ref[pl.ds(pl.multiple_of(front * slab, slab), slab), :]


def anc_kernel(ids, top, rows_out, x_ref, t, l_ref, m_ref):
    count = top.shape[0]
    for c in range(count):
        t[BLK * c : BLK * (c + 1), :] = top[c]
    factor(t, l_ref, x_ref, m_ref)
    at = pl.multiple_of(jnp.minimum(ids[1], count - 1) * BLK, BLK)
    rows_out[...] = l_ref[pl.ds(at, BLK), :]


def update_kernel(ids, dest, col, panel, x_ref, panels, f_out, m0, m1, m2, m3, m4, u_ref, table):
    group = ids[0]
    outs = (m0, m1, m2, m3, m4)
    wide = m0.shape[1] // BLK
    for i in range(len(outs) * wide):
        table[i] = -1
    for j in range(panels.shape[0]):
        diff = dest[group, j] ^ group
        level = sum((diff >= 2**b).astype(jnp.int32) for b in range(1, len(outs)))
        table[level * wide + col[group, j]] = j
    solved = dot(panel[...], x_ref[...], 1, 1)
    f_out[...] = solved
    w = dot(solved, x_ref[...])
    for j in range(panels.shape[0]):
        u_ref[j] = dot(w, panels[j], 1, 1)
    for level, out in enumerate(outs):
        for c in range(wide):
            j = table[level * wide + c]
            out[:, BLK * c : BLK * (c + 1)] = jnp.where(j >= 0, u_ref[jnp.maximum(j, 0)], 0.0)


def final_kernel(ids, rows, front_ref, r0, r1, r2, r3, r4, x_ref, lower, out, t):
    group, front = ids[0], ids[1]
    t[...] = front_ref[...]
    for level, got in enumerate((r0, r1, r2, r3, r4)):
        at = pl.multiple_of(rows[group ^ 2**level, front] * BLK, BLK)
        t[pl.ds(at, BLK), :] = t[pl.ds(at, BLK), :] - got[...]
    out[...] = dot(t[...], x_ref[...], 1, 1)

    @pl.when(front < t.shape[1] // BLK)
    def _():
        out[:BLK, :] = lower[...]


VMEM = pl.BlockSpec(memory_space=pltpu.VMEM)
SMEM = pl.BlockSpec(memory_space=pltpu.SMEM)


def shape(*dims):
    return jax.ShapeDtypeStruct(dims, F32)


def per_device(child_pivot, child_panel, anc_front, dest_list, col_list, row_list):
    fronts = lax.axis_size("front")
    ids = jnp.stack([lax.axis_index("leaf"), lax.axis_index("front")]).astype(jnp.int32)
    slab = child_pivot.shape[1]
    n = child_panel.shape[2]
    levels = lax.axis_size("leaf").bit_length() - 1

    def exchange(value, mask):
        return lax.ppermute(value, "front", [(f, f ^ mask) for f in range(fronts)])

    both = jnp.concatenate([child_panel[0], anc_front[0, 0, :BLK]], 0)
    gathered = lax.all_gather(both, "front", axis=0, tiled=False)

    mine = child_pivot[0]
    pair = jnp.concatenate([mine, exchange(mine, 2)], 0)
    parts = [pair] + [exchange(pair, 2 * k) for k in (2, 4, 6)]
    own = jnp.concatenate(parts, 0)
    other = exchange(own, 1)

    scratch = [pltpu.VMEM((n, n), F32), pltpu.VMEM((n, n), F32), pltpu.VMEM((BLK, 2 * BLK), F32)]
    lower_rows, child_inv = pl.pallas_call(
        child_kernel,
        out_shape=(shape(slab, n), shape(n, n)),
        in_specs=[SMEM, VMEM, VMEM],
        out_specs=(VMEM, VMEM),
        scratch_shapes=scratch,
        name="child_cholesky",
    )(ids, own, other)

    outs = pl.pallas_call(
        update_kernel,
        grid=(1,),
        out_shape=(shape(BLK, n),) * (levels + 1),
        in_specs=[SMEM, SMEM, SMEM, VMEM, VMEM, pl.BlockSpec((fronts, BLK, n), lambda i: (0, 0, 0))],
        out_specs=(VMEM,) * (levels + 1),
        scratch_shapes=[pltpu.VMEM((fronts, BLK, BLK), F32), pltpu.SMEM((levels * (n // BLK),), jnp.int32)],
        name="update",
    )(ids, dest_list, col_list, child_panel[0], child_inv, gathered)
    panel, messages = outs[0], outs[1:]

    arrived = [None] * levels
    for level in (2, 4, 1, 3, 0):
        pairs = [(s, s ^ 2**level) for s in range(lax.axis_size("leaf"))]
        arrived[level] = lax.ppermute(messages[level], "leaf", pairs)

    ids_later, _ = lax.optimization_barrier((ids, messages[0]))
    anc_rows, anc_inv = pl.pallas_call(
        anc_kernel,
        grid=(1,),
        out_shape=(shape(BLK, n), shape(n, n)),
        in_specs=[SMEM, pl.BlockSpec((n // BLK, BLK, n), lambda i: (0, 1, 0))],
        out_specs=(VMEM, VMEM),
        scratch_shapes=scratch,
        name="ancestor_cholesky",
    )(ids_later, gathered)

    anc_out = pl.pallas_call(
        final_kernel,
        out_shape=shape(n, n),
        in_specs=[SMEM, SMEM] + [VMEM] * (levels + 3),
        out_specs=VMEM,
        scratch_shapes=[pltpu.VMEM((n, n), F32)],
        name="finish",
    )(ids, row_list, anc_front[0, 0], *arrived, anc_inv, anc_rows)
    return (lower_rows[None], panel[None], anc_out[None, None])


def solution(mesh):
    in_specs = (
        P("leaf", "front", None),
        P("leaf", "front", None),
        P("leaf", "front", None, None),
        P(),
        P(),
        P(),
    )
    out_specs = (P("leaf", "front", None), P("leaf", "front", None), P("leaf", "front", None, None))
    return jax.shard_map(
        per_device, mesh=mesh, in_specs=in_specs, out_specs=out_specs, check_vma=False
    )
```

```python
import jax
import jax.numpy as jnp
from jax import lax
from jax.experimental import pallas as pl
from jax.experimental.pallas import tpu as pltpu
from jax.sharding import PartitionSpec as P

F32 = jnp.float32
BLK = 128
SUB = 8


def dot(a, b, ca=1, cb=0):
    return lax.dot_general(
        a,
        b,
        (((ca,), (cb,)), ((), ())),
        precision=lax.Precision.HIGHEST,
        preferred_element_type=F32,
    )


def split3(x):
    high = x.astype(jnp.bfloat16).astype(F32)
    rest = x - high
    mid = rest.astype(jnp.bfloat16).astype(F32)
    return high, mid, rest - mid


def eliminate(m_ref, k, here):
    base = SUB * k
    last = base + SUB >= BLK
    ra = [jnp.broadcast_to(here[0][i : i + 1], (SUB, BLK)) for i in range(SUB)]
    rb = [jnp.broadcast_to(here[1][i : i + 1], (SUB, BLK)) for i in range(SUB)]
    d = {}
    for i in range(SUB):
        for j in range(i, SUB):
            d[i, j] = jnp.broadcast_to(ra[i][:, base + j : base + j + 1], (SUB, BLK))
    if not last:
        na = m_ref[base + SUB : base + 2 * SUB, :BLK]
        nb = m_ref[base + SUB : base + 2 * SUB, BLK:]
        c = [jnp.broadcast_to(na[:, base + q : base + q + 1], (SUB, BLK)) for q in range(SUB)]
    sub = lax.broadcasted_iota(jnp.int32, (SUB, BLK), 0)
    ua_all = ub_all = None
    for q in range(SUB):
        s = lax.rsqrt(d[q, q])
        low = {i: d[q, i] * s for i in range(q + 1, SUB)}
        for i in range(q + 1, SUB):
            for j in range(i, SUB):
                d[i, j] = d[i, j] - low[i] * low[j]
        ua = ra[q] * s
        ub = rb[q] * s
        for i in range(q + 1, SUB):
            ra[i] = ra[i] - low[i] * ua
            rb[i] = rb[i] - low[i] * ub
        if not last:
            cq = c[q] * s
            for j in range(q + 1, SUB):
                c[j] = c[j] - cq * low[j]
            na = na - cq * ua
            nb = nb - cq * ub
        ua_all = ua if q == 0 else jnp.where(sub == q, ua, ua_all)
        ub_all = ub if q == 0 else jnp.where(sub == q, ub, ub_all)
    u = jnp.concatenate([ua_all, ub_all], 1)
    m_ref[base : base + SUB, :] = u
    if last:
        return None
    if base + 2 * SUB < BLK:
        hi, mi, lo = split3(u)
        ah, am, al = hi[:, :BLK], mi[:, :BLK], lo[:, :BLK]
        left = jnp.concatenate([ah, ah, am, ah, al, am], 0).astype(jnp.bfloat16)
        right = jnp.concatenate([hi, mi, hi, lo, hi, mi], 0).astype(jnp.bfloat16)
        upd = lax.dot_general(
            left, right, (((0,), (0,)), ((), ())), preferred_element_type=F32
        )
        m_ref[base + 2 * SUB :, :] = m_ref[base + 2 * SUB :, :] - upd[base + 2 * SUB :, :]
    return na, nb


def factor(t, l_ref, x_ref, m_ref):
    n = t.shape[0]
    ri = lax.broadcasted_iota(jnp.int32, (BLK, BLK), 0)
    ci = lax.broadcasted_iota(jnp.int32, (BLK, BLK), 1)
    for r1 in range(BLK, n, BLK):
        zero = jnp.zeros((BLK, n - r1), F32)
        l_ref[r1 - BLK : r1, r1:] = zero
        x_ref[r1 - BLK : r1, r1:] = zero

    def rest(b):
        r0, r1 = b * BLK, (b + 1) * BLK
        inv = m_ref[:, BLK:]
        if r1 < n:
            u = dot(inv, t[r0:r1, r1:])
            for i in range(r1, n, BLK):
                side = u[:, i - r1 : i - r1 + BLK]
                t[i : i + BLK, i:] = t[i : i + BLK, i:] - dot(side, u[:, i - r1 :], 0, 0)
            l_ref[r1:, r0:r1] = u.T
        l_ref[r0:r1, r0:r1] = jnp.where(ci >= ri, m_ref[:, :BLK], 0.0).T
        x_ref[r0:r1, r0:r1] = inv
        if r0:
            x_ref[r0:r1, :r0] = -dot(inv, dot(l_ref[r0:r1, :r0], x_ref[:r0, :r0]))

    def step(b, carry):
        r0 = pl.multiple_of(b * BLK, BLK)
        m_ref[:, :BLK] = t[pl.ds(r0, BLK), pl.ds(r0, BLK)]
        m_ref[:, BLK:] = (ri == ci).astype(F32)
        here = (m_ref[:SUB, :BLK], m_ref[:SUB, BLK:])
        for k in range(BLK // SUB):
            here = eliminate(m_ref, k, here)
        for fixed in range(n // BLK):
            pl.when(b == fixed)(lambda fixed=fixed: rest(fixed))
        return carry

    lax.fori_loop(0, n // BLK, step, 0)


def child_kernel(info, own, other, panel, rows_out, f_out, w_out, t, l_ref, x_ref, m_ref):
    front = info[1]
    z, core = front // 2, front % 2
    slab = rows_out.shape[0]
    for q in range(own.shape[0] // slab):
        at = 2 * slab * (z ^ q)
        mine = pl.multiple_of(at + slab * core, slab)
        theirs = pl.multiple_of(at + slab * (1 - core), slab)
        t[pl.ds(mine, slab), :] = own[slab * q : slab * (q + 1), :]
        t[pl.ds(theirs, slab), :] = other[slab * q : slab * (q + 1), :]
    factor(t, l_ref, x_ref, m_ref)
    rows_out[...] = l_ref[pl.ds(pl.multiple_of(front * slab, slab), slab), :]
    half = x_ref.shape[0] // 2
    first = dot(panel[:, :half], x_ref[:half, :half], 1, 1)
    second = dot(panel[...], x_ref[half:, :], 1, 1)
    f_out[:, :half] = first
    f_out[:, half:] = second
    w_out[:, :half] = dot(f_out[...], x_ref[:, :half])
    w_out[:, half:] = dot(second, x_ref[half:, half:])


def anc_kernel(info, mine, near, across0, across1, rows_out, inv_out, t, l_ref, x_ref, m_ref):
    own = jnp.minimum(info[1], t.shape[0] // BLK - 1)
    for part, mask in ((mine, 0), (near, 2), (across0, 1), (across1, 3)):
        t[pl.ds(pl.multiple_of((own ^ mask) * BLK, BLK), BLK), :] = part[...]
    factor(t, l_ref, x_ref, m_ref)
    at = pl.multiple_of(own * BLK, BLK)
    rows_out[...] = l_ref[pl.ds(at, BLK), :]
    inv_out[...] = x_ref[pl.ds(at, BLK), :]


def update_kernel(info, w, panels, m0, m1, m2, m3, m4, u_ref, table):
    outs = (m0, m1, m2, m3, m4)
    wide = m0.shape[1] // BLK
    fronts = panels.shape[0]
    for i in range(len(outs) * wide):
        table[i] = -1
    for j in range(fronts):
        diff = info[2 + j] ^ info[0]
        level = sum((diff >= 2**b).astype(jnp.int32) for b in range(1, len(outs)))
        table[level * wide + info[2 + fronts + j]] = j
    for j in range(fronts):
        u_ref[j] = dot(w[...], panels[j], 1, 1)
    for level, out in enumerate(outs):
        for c in range(wide):
            j = table[level * wide + c]
            out[:, BLK * c : BLK * (c + 1)] = jnp.where(j >= 0, u_ref[jnp.maximum(j, 0)], 0.0)


def final_kernel(info, front_ref, r0, r1, r2, r3, r4, x_ref, lower, out, t):
    t[...] = front_ref[...]
    for level, got in enumerate((r0, r1, r2, r3, r4)):
        at = pl.multiple_of(info[34 + level] * BLK, BLK)
        t[pl.ds(at, BLK), :] = t[pl.ds(at, BLK), :] - got[...]
    n = t.shape[1]
    half = n // 2
    x = x_ref[...].reshape(n, n)
    out[:, :half] = dot(t[:, :half], x[:half, :half], 1, 1)
    out[:, half:] = dot(t[...], x[half:, :], 1, 1)

    @pl.when(info[1] < t.shape[1] // BLK)
    def _():
        out[:BLK, :] = lower[...]


VMEM = pl.BlockSpec(memory_space=pltpu.VMEM)
SMEM = pl.BlockSpec(memory_space=pltpu.SMEM)


def shape(*dims):
    return jax.ShapeDtypeStruct(dims, F32)


def make_info(group, front, levels, dest_list, col_list, row_list):
    leaves, fronts = dest_list.shape
    width = 2 + 2 * fronts + levels
    lane = jnp.arange(width)
    leaf = jnp.arange(leaves)[:, None]
    wide = jnp.concatenate(
        [
            jnp.zeros((leaves, 2), jnp.int32),
            dest_list,
            col_list,
            jnp.broadcast_to(row_at(row_list, front), (leaves, levels)),
        ],
        1,
    )
    level = lane - (2 + 2 * fronts)
    source = jnp.where(level >= 0, group ^ (1 << jnp.maximum(level, 0)), group)
    picked = jnp.sum(jnp.where(leaf == source[None, :], wide, 0), axis=0)
    return jnp.where(lane == 0, group, jnp.where(lane == 1, front, picked)).astype(jnp.int32)


def row_at(row_list, front):
    lane = jnp.arange(row_list.shape[1])
    return jnp.sum(jnp.where(lane == front, row_list, 0), axis=1, keepdims=True)


def per_device(child_pivot, child_panel, anc_front, dest_list, col_list, row_list):
    fronts = lax.axis_size("front")
    group, front = lax.axis_index("leaf"), lax.axis_index("front")
    slab = child_pivot.shape[1]
    n = child_panel.shape[2]
    levels = lax.axis_size("leaf").bit_length() - 1

    info = make_info(group, front, levels, dest_list, col_list, row_list)

    def pair_up(value, partner):
        pairs = [(2 * z + c, 2 * partner(z) + c) for z in range(fronts // 2) for c in range(2)]
        return lax.ppermute(value, "front", pairs)

    gathered = lax.all_gather(child_panel[0], "front", axis=0, tiled=False)

    mine = child_pivot[0]
    pair = jnp.concatenate([mine, pair_up(mine, lambda z: z ^ 1)], 0)
    top = anc_front[0, 0, :BLK]
    near = lax.ppermute(top, "front", [(f, f ^ 2) for f in range(n // BLK)])
    pair, info = lax.optimization_barrier((pair, info))
    parts = [pair]
    for k in (2, 4, 6):
        parts.append(pair_up(pair, lambda z, k=k: z ^ k))
    across = lax.ppermute(
        jnp.concatenate([top, near], 0), "front", [(f, f ^ 1) for f in range(n // BLK)]
    )
    square = pltpu.VMEM((n, n), F32)
    work = pltpu.VMEM((BLK, 2 * BLK), F32)
    anc_rows, anc_inv = pl.pallas_call(
        anc_kernel,
        grid=(1,),
        out_shape=(shape(BLK, n),) * 2,
        in_specs=[SMEM, VMEM, VMEM]
        + [pl.BlockSpec((BLK, n), lambda i, half=half: (half, 0)) for half in range(2)],
        out_specs=(VMEM, VMEM),
        scratch_shapes=[square, square, square, work],
        name="ancestor_cholesky",
    )(info, top, near, across, across)
    inverses = lax.all_gather(anc_inv, "front", axis=0, tiled=False)

    own = jnp.concatenate(parts, 0)
    other = lax.ppermute(own, "front", [(f, f ^ 1) for f in range(fronts)])
    lower_rows, panel, w = pl.pallas_call(
        child_kernel,
        out_shape=(shape(slab, n), shape(BLK, n), shape(BLK, n)),
        in_specs=[SMEM, VMEM, VMEM, VMEM],
        out_specs=(VMEM,) * 3,
        scratch_shapes=[square, square, square, work],
        name="child_cholesky",
    )(info, own, other, child_panel[0])

    messages = pl.pallas_call(
        update_kernel,
        out_shape=(shape(BLK, n),) * levels,
        in_specs=[SMEM, VMEM, VMEM],
        out_specs=(VMEM,) * levels,
        scratch_shapes=[
            pltpu.VMEM((fronts, BLK, BLK), F32),
            pltpu.SMEM((levels * (n // BLK),), jnp.int32),
        ],
        name="update",
    )(info, w, gathered)

    arrived = [None] * levels
    for level in (2, 4, 1, 3, 0):
        pairs = [(s, s ^ 2**level) for s in range(lax.axis_size("leaf"))]
        arrived[level] = lax.ppermute(messages[level], "leaf", pairs)

    anc_out = pl.pallas_call(
        final_kernel,
        out_shape=shape(n, n),
        grid=(1,),
        in_specs=[SMEM]
        + [VMEM] * (levels + 1)
        + [pl.BlockSpec((n // BLK, BLK, n), lambda i: (0, 0, 0)), VMEM],
        out_specs=VMEM,
        scratch_shapes=[square],
        name="finish",
    )(info, anc_front[0, 0], *arrived, inverses, anc_rows)
    return (lower_rows[None], panel[None], anc_out[None, None])


def solution(mesh):
    in_specs = (
        P("leaf", "front", None),
        P("leaf", "front", None),
        P("leaf", "front", None, None),
        P(),
        P(),
        P(),
    )
    out_specs = (P("leaf", "front", None), P("leaf", "front", None), P("leaf", "front", None, None))

    return jax.shard_map(
        per_device, mesh=mesh, in_specs=in_specs, out_specs=out_specs, check_vma=False
    )
```

```python
import functools

import jax
import jax.numpy as jnp
from jax import lax
from jax.experimental import pallas as pl
from jax.experimental.pallas import tpu as pltpu
from jax.sharding import PartitionSpec as P

F32 = jnp.float32
BLK = 128
SUB = 8


def dot(a, b, ca=1, cb=0):
    return lax.dot_general(
        a,
        b,
        (((ca,), (cb,)), ((), ())),
        precision=lax.Precision.HIGHEST,
        preferred_element_type=F32,
    )


def split3(x):
    high = x.astype(jnp.bfloat16).astype(F32)
    rest = x - high
    mid = rest.astype(jnp.bfloat16).astype(F32)
    return high, mid, rest - mid


def eliminate(m_ref, k, here):
    base = SUB * k
    last = base + SUB >= BLK
    ra = [jnp.broadcast_to(here[0][i : i + 1], (SUB, BLK)) for i in range(SUB)]
    rb = [jnp.broadcast_to(here[1][i : i + 1], (SUB, BLK)) for i in range(SUB)]
    d = {}
    for i in range(SUB):
        for j in range(i, SUB):
            d[i, j] = jnp.broadcast_to(ra[i][:, base + j : base + j + 1], (SUB, BLK))
    if not last:
        na = m_ref[base + SUB : base + 2 * SUB, :BLK]
        nb = m_ref[base + SUB : base + 2 * SUB, BLK:]
        c = [jnp.broadcast_to(na[:, base + q : base + q + 1], (SUB, BLK)) for q in range(SUB)]
    sub = lax.broadcasted_iota(jnp.int32, (SUB, BLK), 0)
    ua_all = ub_all = None
    for q in range(SUB):
        s = lax.rsqrt(d[q, q])
        low = {i: d[q, i] * s for i in range(q + 1, SUB)}
        for i in range(q + 1, SUB):
            for j in range(i, SUB):
                d[i, j] = d[i, j] - low[i] * low[j]
        ua = ra[q] * s
        ub = rb[q] * s
        for i in range(q + 1, SUB):
            ra[i] = ra[i] - low[i] * ua
            rb[i] = rb[i] - low[i] * ub
        if not last:
            cq = c[q] * s
            for j in range(q + 1, SUB):
                c[j] = c[j] - cq * low[j]
            na = na - cq * ua
            nb = nb - cq * ub
        ua_all = ua if q == 0 else jnp.where(sub == q, ua, ua_all)
        ub_all = ub if q == 0 else jnp.where(sub == q, ub, ub_all)
    u = jnp.concatenate([ua_all, ub_all], 1)
    m_ref[base : base + SUB, :] = u
    if last:
        return None
    if base + 2 * SUB < BLK:
        hi, mi, lo = split3(u)
        ah, am, al = hi[:, :BLK], mi[:, :BLK], lo[:, :BLK]
        left = jnp.concatenate([ah, ah, am, ah, al, am], 0).astype(jnp.bfloat16)
        right = jnp.concatenate([hi, mi, hi, lo, hi, mi], 0).astype(jnp.bfloat16)
        upd = lax.dot_general(
            left, right, (((0,), (0,)), ((), ())), preferred_element_type=F32
        )
        m_ref[base + 2 * SUB :, :] = m_ref[base + 2 * SUB :, :] - upd[base + 2 * SUB :, :]
    return na, nb


def factor(t, l_ref, x_ref, m_ref):
    n = t.shape[0]
    ri = lax.broadcasted_iota(jnp.int32, (BLK, BLK), 0)
    ci = lax.broadcasted_iota(jnp.int32, (BLK, BLK), 1)
    for r1 in range(BLK, n, BLK):
        zero = jnp.zeros((BLK, n - r1), F32)
        l_ref[r1 - BLK : r1, r1:] = zero
        x_ref[r1 - BLK : r1, r1:] = zero

    def rest(b):
        r0, r1 = b * BLK, (b + 1) * BLK
        inv = m_ref[:, BLK:]
        if r1 < n:
            u = dot(inv, t[r0:r1, r1:])
            for i in range(r1, n, BLK):
                side = u[:, i - r1 : i - r1 + BLK]
                t[i : i + BLK, i:] = t[i : i + BLK, i:] - dot(side, u[:, i - r1 :], 0, 0)
            l_ref[r1:, r0:r1] = u.T
        l_ref[r0:r1, r0:r1] = jnp.where(ci >= ri, m_ref[:, :BLK], 0.0).T
        x_ref[r0:r1, r0:r1] = inv
        if r0:
            x_ref[r0:r1, :r0] = -dot(inv, dot(l_ref[r0:r1, :r0], x_ref[:r0, :r0]))

    def step(b, carry):
        r0 = pl.multiple_of(b * BLK, BLK)
        m_ref[:, :BLK] = t[pl.ds(r0, BLK), pl.ds(r0, BLK)]
        m_ref[:, BLK:] = (ri == ci).astype(F32)
        here = (m_ref[:SUB, :BLK], m_ref[:SUB, BLK:])
        for k in range(BLK // SUB):
            here = eliminate(m_ref, k, here)
        for fixed in range(n // BLK):
            pl.when(b == fixed)(lambda fixed=fixed: rest(fixed))
        return carry

    lax.fori_loop(0, n // BLK, step, 0)


def child_kernel(info, own, other, panel, rows_out, f_out, w_out, t, l_ref, x_ref, m_ref):
    front = info[1]
    z, core = front // 2, front % 2
    slab = rows_out.shape[0]
    for q in range(own.shape[0] // slab):
        at = 2 * slab * (z ^ q)
        mine = pl.multiple_of(at + slab * core, slab)
        theirs = pl.multiple_of(at + slab * (1 - core), slab)
        t[pl.ds(mine, slab), :] = own[slab * q : slab * (q + 1), :]
        t[pl.ds(theirs, slab), :] = other[slab * q : slab * (q + 1), :]
    factor(t, l_ref, x_ref, m_ref)
    rows_out[...] = l_ref[pl.ds(pl.multiple_of(front * slab, slab), slab), :]
    half = x_ref.shape[0] // 2
    first = dot(panel[:, :half], x_ref[:half, :half], 1, 1)
    second = dot(panel[...], x_ref[half:, :], 1, 1)
    f_out[:, :half] = first
    f_out[:, half:] = second
    w_out[:, :half] = dot(f_out[...], x_ref[:, :half])
    w_out[:, half:] = dot(second, x_ref[half:, half:])


def anc_kernel(info, mine, near, across0, across1, rows_out, inv_out, t, l_ref, x_ref, m_ref):
    own = jnp.minimum(info[1], t.shape[0] // BLK - 1)
    for part, mask in ((mine, 0), (near, 2), (across0, 1), (across1, 3)):
        t[pl.ds(pl.multiple_of((own ^ mask) * BLK, BLK), BLK), :] = part[...]
    factor(t, l_ref, x_ref, m_ref)
    at = pl.multiple_of(own * BLK, BLK)
    rows_out[...] = l_ref[pl.ds(at, BLK), :]
    inv_out[...] = x_ref[pl.ds(at, BLK), :]


def halves(x):
    high = x.astype(jnp.bfloat16)
    return high, (x - high.astype(F32)).astype(jnp.bfloat16)


def dot_halves(a, b):
    def part(x, y):
        return lax.dot_general(x, y, (((1,), (1,)), ((), ())), preferred_element_type=F32)

    return part(a[0], b[0]) + (part(a[0], b[1]) + part(a[1], b[0]))


def block_table(info, table, wide, levels, fronts):
    for i in range(levels * wide):
        table[i] = -1
    for j in range(fronts):
        diff = info[2 + j] ^ info[0]
        level = sum((diff >= 2**b).astype(jnp.int32) for b in range(1, levels))
        table[level * wide + info[2 + fronts + j]] = j


def update_kernel(chosen, levels, info, w, panels, *refs):
    outs, (table, u_ref) = refs[: len(chosen)], refs[len(chosen) :]
    wide = outs[0].shape[1] // BLK
    fronts = panels.shape[0]
    block_table(info, table, wide, levels, fronts)
    left = halves(w[...])
    for j in range(fronts):
        u_ref[j] = dot_halves(left, halves(panels[j]))
    for level, out in zip(chosen, outs):
        for c in range(wide):
            j = table[level * wide + c]
            out[:, BLK * c : BLK * (c + 1)] = jnp.where(j >= 0, u_ref[jnp.maximum(j, 0)], 0.0)


def final_kernel(info, front_ref, r0, r1, r2, r3, r4, x_ref, lower, out, t):
    t[...] = front_ref[...]
    for level, got in enumerate((r0, r1, r2, r3, r4)):
        at = pl.multiple_of(info[34 + level] * BLK, BLK)
        t[pl.ds(at, BLK), :] = t[pl.ds(at, BLK), :] - got[...]
    n = t.shape[1]
    half = n // 2
    x = x_ref[...].reshape(n, n)
    out[:, :half] = dot_halves(halves(t[:, :half]), halves(x[:half, :half]))
    out[:, half:] = dot_halves(halves(t[...]), halves(x[half:, :]))

    @pl.when(info[1] < t.shape[1] // BLK)
    def _():
        out[:BLK, :] = lower[...]


VMEM = pl.BlockSpec(memory_space=pltpu.VMEM)
SMEM = pl.BlockSpec(memory_space=pltpu.SMEM)


def shape(*dims):
    return jax.ShapeDtypeStruct(dims, F32)


def make_info(group, front, levels, dest_list, col_list, row_list):
    leaves, fronts = dest_list.shape
    width = 2 + 2 * fronts + levels
    lane = jnp.arange(width)
    leaf = jnp.arange(leaves)[:, None]
    wide = jnp.concatenate(
        [
            jnp.zeros((leaves, 2), jnp.int32),
            dest_list,
            col_list,
            jnp.broadcast_to(row_at(row_list, front), (leaves, levels)),
        ],
        1,
    )
    level = lane - (2 + 2 * fronts)
    source = jnp.where(level >= 0, group ^ (1 << jnp.maximum(level, 0)), group)
    picked = jnp.sum(jnp.where(leaf == source[None, :], wide, 0), axis=0)
    return jnp.where(lane == 0, group, jnp.where(lane == 1, front, picked)).astype(jnp.int32)


def row_at(row_list, front):
    lane = jnp.arange(row_list.shape[1])
    return jnp.sum(jnp.where(lane == front, row_list, 0), axis=1, keepdims=True)


def per_device(child_pivot, child_panel, anc_front, dest_list, col_list, row_list):
    fronts = lax.axis_size("front")
    group, front = lax.axis_index("leaf"), lax.axis_index("front")
    slab = child_pivot.shape[1]
    n = child_panel.shape[2]
    levels = lax.axis_size("leaf").bit_length() - 1

    info = make_info(group, front, levels, dest_list, col_list, row_list)

    def pair_up(value, partner):
        pairs = [(2 * z + c, 2 * partner(z) + c) for z in range(fronts // 2) for c in range(2)]
        return lax.ppermute(value, "front", pairs)

    gathered = lax.all_gather(child_panel[0], "front", axis=0, tiled=False)

    mine = child_pivot[0]
    pair = jnp.concatenate([mine, pair_up(mine, lambda z: z ^ 1)], 0)
    top = anc_front[0, 0, :BLK]
    near = lax.ppermute(top, "front", [(f, f ^ 2) for f in range(n // BLK)])
    pair, info = lax.optimization_barrier((pair, info))
    parts = [pair]
    for k in (2, 4, 6):
        parts.append(pair_up(pair, lambda z, k=k: z ^ k))
    across = lax.ppermute(
        jnp.concatenate([top, near], 0), "front", [(f, f ^ 1) for f in range(n // BLK)]
    )
    square = pltpu.VMEM((n, n), F32)
    work = pltpu.VMEM((BLK, 2 * BLK), F32)
    anc_rows, anc_inv = pl.pallas_call(
        anc_kernel,
        grid=(1,),
        out_shape=(shape(BLK, n),) * 2,
        in_specs=[SMEM, VMEM, VMEM]
        + [pl.BlockSpec((BLK, n), lambda i, half=half: (half, 0)) for half in range(2)],
        out_specs=(VMEM, VMEM),
        scratch_shapes=[square, square, square, work],
        name="ancestor_cholesky",
    )(info, top, near, across, across)
    inverses = lax.all_gather(anc_inv, "front", axis=0, tiled=False)

    own = jnp.concatenate(parts, 0)
    other = lax.ppermute(own, "front", [(f, f ^ 1) for f in range(fronts)])
    lower_rows, panel, w = pl.pallas_call(
        child_kernel,
        out_shape=(shape(slab, n), shape(BLK, n), shape(BLK, n)),
        in_specs=[SMEM, VMEM, VMEM, VMEM],
        out_specs=(VMEM,) * 3,
        scratch_shapes=[square, square, square, work],
        name="child_cholesky",
    )(info, own, other, child_panel[0])

    table = pltpu.SMEM((levels * (n // BLK),), jnp.int32)
    messages = [None] * levels
    chosen = (2, 1, 4, 3, 0)
    others = pl.pallas_call(
        functools.partial(update_kernel, chosen, levels),
        out_shape=(shape(BLK, n),) * len(chosen),
        in_specs=[SMEM, VMEM, VMEM],
        out_specs=(VMEM,) * len(chosen),
        scratch_shapes=[table, pltpu.VMEM((fronts, BLK, BLK), F32)],
        name="update",
    )(info, w, gathered)
    for level, message in zip(chosen, others):
        messages[level] = message

    arrived = [None] * levels
    for level in (2, 4, 1, 3, 0):
        pairs = [(s, s ^ 2**level) for s in range(lax.axis_size("leaf"))]
        arrived[level] = lax.ppermute(messages[level], "leaf", pairs)

    anc_out = pl.pallas_call(
        final_kernel,
        out_shape=shape(n, n),
        grid=(1,),
        in_specs=[SMEM]
        + [VMEM] * (levels + 1)
        + [pl.BlockSpec((n // BLK, BLK, n), lambda i: (0, 0, 0)), VMEM],
        out_specs=VMEM,
        scratch_shapes=[square],
        name="finish",
    )(info, anc_front[0, 0], *arrived, inverses, anc_rows)
    return (lower_rows[None], panel[None], anc_out[None, None])


def solution(mesh):
    in_specs = (
        P("leaf", "front", None),
        P("leaf", "front", None),
        P("leaf", "front", None, None),
        P(),
        P(),
        P(),
    )
    out_specs = (P("leaf", "front", None), P("leaf", "front", None), P("leaf", "front", None, None))

    return jax.shard_map(
        per_device, mesh=mesh, in_specs=in_specs, out_specs=out_specs, check_vma=False
    )
```

```python
import functools

import jax
import jax.numpy as jnp
from jax import lax
from jax.experimental import pallas as pl
from jax.experimental.pallas import tpu as pltpu
from jax.sharding import PartitionSpec as P

F32 = jnp.float32
BLK = 128
SUB = 8


def dot(a, b, ca=1, cb=0):
    return lax.dot_general(
        a,
        b,
        (((ca,), (cb,)), ((), ())),
        precision=lax.Precision.HIGHEST,
        preferred_element_type=F32,
    )


def split3(x):
    high = x.astype(jnp.bfloat16).astype(F32)
    rest = x - high
    mid = rest.astype(jnp.bfloat16).astype(F32)
    return high, mid, rest - mid


def eliminate(m_ref, k, here):
    base = SUB * k
    last = base + SUB >= BLK
    ra = [jnp.broadcast_to(here[0][i : i + 1], (SUB, BLK)) for i in range(SUB)]
    rb = [jnp.broadcast_to(here[1][i : i + 1], (SUB, BLK)) for i in range(SUB)]
    d = {}
    for i in range(SUB):
        for j in range(i, SUB):
            d[i, j] = jnp.broadcast_to(ra[i][:, base + j : base + j + 1], (SUB, BLK))
    if not last:
        na = m_ref[base + SUB : base + 2 * SUB, :BLK]
        nb = m_ref[base + SUB : base + 2 * SUB, BLK:]
        c = [jnp.broadcast_to(na[:, base + q : base + q + 1], (SUB, BLK)) for q in range(SUB)]
    sub = lax.broadcasted_iota(jnp.int32, (SUB, BLK), 0)
    ua_all = ub_all = None
    for q in range(SUB):
        s = lax.rsqrt(d[q, q])
        low = {i: d[q, i] * s for i in range(q + 1, SUB)}
        for i in range(q + 1, SUB):
            for j in range(i, SUB):
                d[i, j] = d[i, j] - low[i] * low[j]
        ua = ra[q] * s
        ub = rb[q] * s
        for i in range(q + 1, SUB):
            ra[i] = ra[i] - low[i] * ua
            rb[i] = rb[i] - low[i] * ub
        if not last:
            cq = c[q] * s
            for j in range(q + 1, SUB):
                c[j] = c[j] - cq * low[j]
            na = na - cq * ua
            nb = nb - cq * ub
        ua_all = ua if q == 0 else jnp.where(sub == q, ua, ua_all)
        ub_all = ub if q == 0 else jnp.where(sub == q, ub, ub_all)
    u = jnp.concatenate([ua_all, ub_all], 1)
    m_ref[base : base + SUB, :] = u
    if last:
        return None
    if base + 2 * SUB < BLK:
        hi, mi, lo = split3(u)
        ah, am, al = hi[:, :BLK], mi[:, :BLK], lo[:, :BLK]
        left = jnp.concatenate([ah, ah, am, ah, al, am], 0).astype(jnp.bfloat16)
        right = jnp.concatenate([hi, mi, hi, lo, hi, mi], 0).astype(jnp.bfloat16)
        upd = lax.dot_general(
            left, right, (((0,), (0,)), ((), ())), preferred_element_type=F32
        )
        m_ref[base + 2 * SUB :, :] = m_ref[base + 2 * SUB :, :] - upd[base + 2 * SUB :, :]
    return na, nb


def factor(t, l_ref, x_ref, m_ref):
    n = t.shape[0]
    ri = lax.broadcasted_iota(jnp.int32, (BLK, BLK), 0)
    ci = lax.broadcasted_iota(jnp.int32, (BLK, BLK), 1)
    for r1 in range(BLK, n, BLK):
        zero = jnp.zeros((BLK, n - r1), F32)
        l_ref[r1 - BLK : r1, r1:] = zero
        x_ref[r1 - BLK : r1, r1:] = zero

    def rest(b):
        r0, r1 = b * BLK, (b + 1) * BLK
        inv = m_ref[:, BLK:]
        if r1 < n:
            u = dot(inv, t[r0:r1, r1:])
            for i in range(r1, n, BLK):
                side = u[:, i - r1 : i - r1 + BLK]
                t[i : i + BLK, i:] = t[i : i + BLK, i:] - dot(side, u[:, i - r1 :], 0, 0)
            l_ref[r1:, r0:r1] = u.T
        l_ref[r0:r1, r0:r1] = jnp.where(ci >= ri, m_ref[:, :BLK], 0.0).T
        x_ref[r0:r1, r0:r1] = inv
        if r0:
            x_ref[r0:r1, :r0] = -dot(inv, dot(l_ref[r0:r1, :r0], x_ref[:r0, :r0]))

    def step(b, carry):
        r0 = pl.multiple_of(b * BLK, BLK)
        m_ref[:, :BLK] = t[pl.ds(r0, BLK), pl.ds(r0, BLK)]
        m_ref[:, BLK:] = (ri == ci).astype(F32)
        here = (m_ref[:SUB, :BLK], m_ref[:SUB, BLK:])
        for k in range(BLK // SUB):
            here = eliminate(m_ref, k, here)
        for fixed in range(n // BLK):
            pl.when(b == fixed)(lambda fixed=fixed: rest(fixed))
        return carry

    lax.fori_loop(0, n // BLK, step, 0)


def child_kernel(info, own, other, panel, rows_out, f_out, w_out, t, l_ref, x_ref, m_ref):
    front = info[1]
    z, core = front // 2, front % 2
    slab = rows_out.shape[0]
    for q in range(own.shape[0] // slab):
        at = 2 * slab * (z ^ q)
        mine = pl.multiple_of(at + slab * core, slab)
        theirs = pl.multiple_of(at + slab * (1 - core), slab)
        t[pl.ds(mine, slab), :] = own[slab * q : slab * (q + 1), :]
        t[pl.ds(theirs, slab), :] = other[slab * q : slab * (q + 1), :]
    factor(t, l_ref, x_ref, m_ref)
    rows_out[...] = l_ref[pl.ds(pl.multiple_of(front * slab, slab), slab), :]
    half = x_ref.shape[0] // 2
    first = dot(panel[:, :half], x_ref[:half, :half], 1, 1)
    second = dot(panel[...], x_ref[half:, :], 1, 1)
    f_out[:, :half] = first
    f_out[:, half:] = second
    w_out[:, :half] = dot(f_out[...], x_ref[:, :half])
    w_out[:, half:] = dot(second, x_ref[half:, half:])


def anc_kernel(place, mine, near, across0, across1, rows_out, inv_out, t, l_ref, x_ref, m_ref):
    own = jnp.minimum(place[0], t.shape[0] // BLK - 1)
    for part, mask in ((mine, 0), (near, 2), (across0, 1), (across1, 3)):
        t[pl.ds(pl.multiple_of((own ^ mask) * BLK, BLK), BLK), :] = part[...]
    factor(t, l_ref, x_ref, m_ref)
    at = pl.multiple_of(own * BLK, BLK)
    rows_out[...] = l_ref[pl.ds(at, BLK), :]
    inv_out[...] = x_ref[pl.ds(at, BLK), :]


def halves(x):
    high = x.astype(jnp.bfloat16)
    return high, (x - high.astype(F32)).astype(jnp.bfloat16)


def dot_halves(a, b):
    def part(x, y):
        return lax.dot_general(x, y, (((1,), (1,)), ((), ())), preferred_element_type=F32)

    return part(a[0], b[0]) + (part(a[0], b[1]) + part(a[1], b[0]))


def block_table(info, table, wide, levels, fronts):
    for i in range(levels * wide):
        table[i] = -1
    for j in range(fronts):
        diff = info[2 + j] ^ info[0]
        level = sum((diff >= 2**b).astype(jnp.int32) for b in range(1, levels))
        table[level * wide + info[2 + fronts + j]] = j


def update_kernel(chosen, levels, info, w, panels, *refs):
    outs, (table, u_ref) = refs[: len(chosen)], refs[len(chosen) :]
    wide = outs[0].shape[1] // BLK
    fronts = panels.shape[0]
    block_table(info, table, wide, levels, fronts)
    left = halves(w[...])
    for j in range(fronts):
        u_ref[j] = dot_halves(left, halves(panels[j]))
    for level, out in zip(chosen, outs):
        for c in range(wide):
            j = table[level * wide + c]
            out[:, BLK * c : BLK * (c + 1)] = jnp.where(j >= 0, u_ref[jnp.maximum(j, 0)], 0.0)


def final_kernel(info, front_ref, r0, r1, r2, r3, r4, x_ref, lower, out, t):
    t[...] = front_ref[...]
    for level, got in enumerate((r0, r1, r2, r3, r4)):
        at = pl.multiple_of(info[34 + level] * BLK, BLK)
        t[pl.ds(at, BLK), :] = t[pl.ds(at, BLK), :] - got[...]
    n = t.shape[1]
    half = n // 2
    x = x_ref[...].reshape(n, n)
    out[:, :half] = dot_halves(halves(t[:, :half]), halves(x[:half, :half]))
    out[:, half:] = dot_halves(halves(t[...]), halves(x[half:, :]))

    @pl.when(info[1] < t.shape[1] // BLK)
    def _():
        out[:BLK, :] = lower[...]


VMEM = pl.BlockSpec(memory_space=pltpu.VMEM)
SMEM = pl.BlockSpec(memory_space=pltpu.SMEM)


def shape(*dims):
    return jax.ShapeDtypeStruct(dims, F32)


def make_info(group, front, levels, dest_list, col_list, row_list):
    leaves, fronts = dest_list.shape
    width = 2 + 2 * fronts + levels
    lane = jnp.arange(width)
    leaf = jnp.arange(leaves)[:, None]
    wide = jnp.concatenate(
        [
            jnp.zeros((leaves, 2), jnp.int32),
            dest_list,
            col_list,
            jnp.broadcast_to(row_at(row_list, front), (leaves, levels)),
        ],
        1,
    )
    level = lane - (2 + 2 * fronts)
    source = jnp.where(level >= 0, group ^ (1 << jnp.maximum(level, 0)), group)
    picked = jnp.sum(jnp.where(leaf == source[None, :], wide, 0), axis=0)
    return jnp.where(lane == 0, group, jnp.where(lane == 1, front, picked)).astype(jnp.int32)


def row_at(row_list, front):
    lane = jnp.arange(row_list.shape[1])
    return jnp.sum(jnp.where(lane == front, row_list, 0), axis=1, keepdims=True)


def per_device(child_pivot, child_panel, anc_front, dest_list, col_list, row_list):
    fronts = lax.axis_size("front")
    group, front = lax.axis_index("leaf"), lax.axis_index("front")
    slab = child_pivot.shape[1]
    n = child_panel.shape[2]
    levels = lax.axis_size("leaf").bit_length() - 1

    place = jnp.full((1,), front, jnp.int32)

    def pair_up(value, partner):
        pairs = [(2 * z + c, 2 * partner(z) + c) for z in range(fronts // 2) for c in range(2)]
        return lax.ppermute(value, "front", pairs)

    gathered = lax.all_gather(child_panel[0], "front", axis=0, tiled=False)

    mine = child_pivot[0]
    beside = pair_up(mine, lambda z: z ^ 1)
    pair = jnp.concatenate([mine, beside], 0)
    top = anc_front[0, 0, :BLK]
    near = lax.ppermute(top, "front", [(f, f ^ 2) for f in range(n // BLK)])
    parts = [pair]
    for k in (2, 4, 6):
        parts.append(pair_up(pair, lambda z, k=k: z ^ k))
    across = lax.ppermute(
        jnp.concatenate([top, near], 0), "front", [(f, f ^ 1) for f in range(n // BLK)]
    )
    square = pltpu.VMEM((n, n), F32)
    work = pltpu.VMEM((BLK, 2 * BLK), F32)
    anc_rows, anc_inv = pl.pallas_call(
        anc_kernel,
        grid=(1,),
        out_shape=(shape(BLK, n),) * 2,
        in_specs=[SMEM, VMEM, VMEM]
        + [pl.BlockSpec((BLK, n), lambda i, half=half: (half, 0)) for half in range(2)],
        out_specs=(VMEM, VMEM),
        scratch_shapes=[square, square, square, work],
        name="ancestor_cholesky",
    )(place, top, near, across, across)
    inverses = lax.all_gather(anc_inv, "front", axis=0, tiled=False)

    own = jnp.concatenate(parts, 0)
    own, dest_list, col_list, row_list = lax.optimization_barrier(
        (own, dest_list, col_list, row_list)
    )
    other = lax.ppermute(own, "front", [(f, f ^ 1) for f in range(fronts)])
    info = make_info(group, front, levels, dest_list, col_list, row_list)
    lower_rows, panel, w = pl.pallas_call(
        child_kernel,
        out_shape=(shape(slab, n), shape(BLK, n), shape(BLK, n)),
        in_specs=[SMEM, VMEM, VMEM, VMEM],
        out_specs=(VMEM,) * 3,
        scratch_shapes=[square, square, square, work],
        name="child_cholesky",
    )(info, own, other, child_panel[0])

    table = pltpu.SMEM((levels * (n // BLK),), jnp.int32)
    messages = [None] * levels
    chosen = (2, 1, 4, 3, 0)
    others = pl.pallas_call(
        functools.partial(update_kernel, chosen, levels),
        out_shape=(shape(BLK, n),) * len(chosen),
        in_specs=[SMEM, VMEM, VMEM],
        out_specs=(VMEM,) * len(chosen),
        scratch_shapes=[table, pltpu.VMEM((fronts, BLK, BLK), F32)],
        name="update",
    )(info, w, gathered)
    for level, message in zip(chosen, others):
        messages[level] = message

    arrived = [None] * levels
    for level in (2, 4, 1, 3, 0):
        pairs = [(s, s ^ 2**level) for s in range(lax.axis_size("leaf"))]
        arrived[level] = lax.ppermute(messages[level], "leaf", pairs)

    anc_out = pl.pallas_call(
        final_kernel,
        out_shape=shape(n, n),
        grid=(1,),
        in_specs=[SMEM]
        + [VMEM] * (levels + 1)
        + [pl.BlockSpec((n // BLK, BLK, n), lambda i: (0, 0, 0)), VMEM],
        out_specs=VMEM,
        scratch_shapes=[square],
        name="finish",
    )(info, anc_front[0, 0], *arrived, inverses, anc_rows)
    return (lower_rows[None], panel[None], anc_out[None, None])


def solution(mesh):
    in_specs = (
        P("leaf", "front", None),
        P("leaf", "front", None),
        P("leaf", "front", None, None),
        P(),
        P(),
        P(),
    )
    out_specs = (P("leaf", "front", None), P("leaf", "front", None), P("leaf", "front", None, None))

    return jax.shard_map(
        per_device, mesh=mesh, in_specs=in_specs, out_specs=out_specs, check_vma=False
    )
```
